32 devices in a mesh: gx: 4 (over y, x), gy: 4 (over z), ga: 2 (over core).
Axes of the slice: x: 2, y: 2, z: 4, core: 2. Of those that a mesh axis runs over, the one named last changes fastest.
Arguments:
- fields: float32 [5, 16, 64, 1024], P(None, 'ga', 'gx', 'gy'), may hold values from -6 to 6
- stiffness: float32 [16, 64, 1024], P('ga', 'gx', 'gy'), may hold values from 0.25 to 4
- lift_weight: float32 [5, 32], replicated, may hold values from -2.5 to 2.5
- lift_bias: float32 [32], replicated, may hold values from -3 to 3
- mix_weight: bfloat16 [32, 32], replicated, may hold values from -0.5 to 0.5
- spectral_weight: float32 [8, 32, 32, 32, 128], P('ga', 'gy', None, 'gx'), may hold values from -0.48 to 0.48
- output_bias: float32 [32], replicated, may hold values from -3 to 3
Outputs:
- layer_out: bfloat16 [16, 32, 32, 512], P('ga', None, 'gx', 'gy')
The draws below stay inside these ranges and needn't reach their ends.
All inputs are finite; a program needn't handle non-finite values.
Results may differ from the reference program's by a relative error of at most 0.01.
Values may be sent and summed in bfloat16 or wider, within the bound.
A program may use at most 128 MiB of HBM per device.

```python
import math
import jax
import jax.numpy as jnp
from jax import lax

NZ = 16
STEPS = 3
C = 32
MX = 32
MY = 64
MZ = 8
NX = 64
NY = 1024


wave_count = 48


def wave_tables(key, term_count):
    key_list = jax.random.split(key, 4)
    east_reach = max(1, min(MX // 2 - 1, NX // 16))
    north_reach = max(1, min(MY // 2 - 1, NY // 16))
    east_wave = jax.random.randint(key_list[0], (term_count,), -east_reach, east_reach + 1, dtype=jnp.int32)
    north_wave = jax.random.randint(key_list[1], (term_count,), -north_reach, north_reach + 1, dtype=jnp.int32)
    east_shift = jax.random.uniform(key_list[2], (term_count, 1), jnp.float32, 0.0, 2.0 * math.pi)
    north_shift = jax.random.uniform(key_list[3], (term_count, 1), jnp.float32, 0.0, 2.0 * math.pi)
    east_index = jnp.arange(NX, dtype=jnp.int32)
    north_index = jnp.arange(NY, dtype=jnp.int32)
    east_angle = jnp.mod(east_wave[:, None] * east_index[None, :], NX).astype(jnp.float32) * (2.0 * math.pi / NX) + east_shift
    north_angle = jnp.mod(north_wave[:, None] * north_index[None, :], NY).astype(jnp.float32) * (2.0 * math.pi / NY) + north_shift
    return (jnp.cos(east_angle), jnp.sin(east_angle), jnp.cos(north_angle), jnp.sin(north_angle))


def smooth_field(key, amplitude):
    east_cos, east_sin, north_cos, north_sin = wave_tables(key, amplitude.shape[-1])
    first = jnp.einsum('...j,jx,jy->...xy', amplitude, east_cos, north_cos)
    second = jnp.einsum('...j,jx,jy->...xy', amplitude, east_sin, north_sin)
    return first - second


def draw_fields(key, part):
    key_list = jax.random.split(key, 3)
    depth_index = jnp.arange(NZ, dtype=jnp.int32)
    orders = jnp.arange(5, dtype=jnp.int32)
    depth_angle = jnp.mod(orders[:, None] * depth_index[None, :], NZ).astype(jnp.float32) * (2.0 * math.pi / NZ)
    profile = jnp.stack([jnp.cos(depth_angle), jnp.sin(depth_angle)], axis=1)
    target = 2.5
    jagged = jax.random.normal(key_list[2], (5, NZ, NX, NY), jnp.float32)
    weights_depth = jax.random.normal(key_list[0], (5, wave_count, 5, 2), jnp.float32) * (target / math.sqrt(2.5 * wave_count))
    amplitude = jnp.einsum('fjkp,kpz->fzj', weights_depth, profile)
    smooth = smooth_field(key_list[1], amplitude)
    return jnp.clip(smooth + jagged, -6.0, 6.0)


def draw_stiffness(key, part):
    key_list = jax.random.split(key, 3)
    amplitude = jax.random.normal(key_list[0], (NZ, wave_count), jnp.float32) * (1.0 / math.sqrt(0.5 * wave_count))
    smooth = smooth_field(key_list[1], amplitude)
    jagged = jax.random.uniform(key_list[2], (NZ, NX, NY), jnp.float32, -1.0, 1.0)
    level = 0.5 + 0.3 * smooth + 0.25 * jagged
    level = jnp.clip(level, 0.0, 1.0)
    return 0.25 * jnp.exp(level * math.log(16.0))


def block_levels(rng, shape, pieces, smallest, top_value):
    factor_of, own = 1.0, jax.random.fold_in(rng, 6)
    for position, blocks in pieces:
        heights = jnp.exp(jax.random.uniform(jax.random.fold_in(own, position), (blocks,), jnp.float32, smallest / len(pieces), top_value / len(pieces)))
        factor_of = factor_of * jnp.repeat(heights, shape[position] // blocks).reshape([-1 if axis == position else 1 for axis in range(len(shape))])
    return factor_of


def gaussian(rng, dims, width, bound, cuts=(), kind=jnp.bfloat16):
    result = width * jax.random.normal(rng, dims, jnp.float32)
    if cuts:
        result = result * block_levels(rng, dims, cuts, -0.22, 0.18)
    return jnp.clip(result, -bound, bound).astype(kind)


def setup_inputs(seed: int = 0) -> dict:
    keys = jax.random.split(jax.random.key(seed), 8)
    return {
        "fields": draw_fields(jax.random.fold_in(keys[7], 71), 0),
        "stiffness": draw_stiffness(jax.random.fold_in(keys[7], 71), 0),
        "lift_weight": gaussian(keys[2], (5, C), 5 ** -0.5, 2.5, (), jnp.float32),
        "lift_bias": gaussian(keys[3], (C,), 0.5, 3.0, (), jnp.float32),
        "mix_weight": gaussian(keys[4], (C, C), (4 * C) ** -0.5, 0.5),
        "spectral_weight": gaussian(keys[5], (MZ, MX, C, C, 2 * MY), 0.08, 0.48, ((0, 2), (1, 4), (3, 4)), jnp.float32),
        "output_bias": gaussian(keys[6], (C,), 0.5, 3.0, (), jnp.float32),
    }


courant_half = 0.1
smooth_half = 0.15
mean_flow = (0.3, -0.2, 0.1)
highest = lax.Precision.HIGHEST

def step_interior(padded, stiff_part):
    center = padded[:, 1:-1, 1:-1, 1:-1]
    upper_depth = padded[:, 2:, 1:-1, 1:-1]
    lower_depth = padded[:, :-2, 1:-1, 1:-1]
    upper_east = padded[:, 1:-1, 2:, 1:-1]
    lower_east = padded[:, 1:-1, :-2, 1:-1]
    upper_north = padded[:, 1:-1, 1:-1, 2:]
    lower_north = padded[:, 1:-1, 1:-1, :-2]
    slope_depth = upper_depth - lower_depth
    slope_east = upper_east - lower_east
    slope_north = upper_north - lower_north
    curvature = upper_depth + lower_depth + upper_east + lower_east + upper_north + lower_north - 6.0 * center
    transport = mean_flow[0] * slope_east + mean_flow[1] * slope_north + mean_flow[2] * slope_depth
    diverge = slope_east[1] + slope_north[2] + slope_depth[3]
    coupling = jnp.stack([diverge, slope_east[4], slope_north[4], slope_depth[4], stiff_part * diverge])
    return center - courant_half * (transport + coupling) + smooth_half * curvature

def coarsen(fields_now):
    extent = fields_now.shape
    blocks = fields_now.reshape(extent[0], extent[1], extent[2] // 2, 2, extent[3] // 2, 2)
    return 0.25 * (blocks[:, :, :, 0, :, 0] + blocks[:, :, :, 1, :, 0] + blocks[:, :, :, 0, :, 1] + blocks[:, :, :, 1, :, 1])

def angles(frequencies, points, length):
    product = jnp.mod(frequencies[:, None] * points[None, :], length)
    return product.astype(jnp.float32) * (2.0 * math.pi / length)

def centered(number):
    return jnp.arange(number, dtype=jnp.int32) - number // 2

def forward_east_table(points, length, mode_count):
    phases = angles(centered(mode_count), points, length)
    factor = 1.0 / math.sqrt(length)
    return (jnp.stack([jnp.cos(phases).T, -jnp.sin(phases).T], axis=1) * factor).astype(jnp.bfloat16)

def forward_north_table(points, length, mode_count):
    phases = angles(centered(mode_count), points, length)
    factor = 1.0 / math.sqrt(length)
    cosines = jnp.cos(phases).T * factor
    sines = jnp.sin(phases).T * factor
    return jnp.stack([jnp.concatenate([cosines, -sines], axis=1), jnp.concatenate([sines, cosines], axis=1)], axis=0)

def inverse_north_table(points, length, mode_count):
    phases = angles(centered(mode_count), points, length)
    factor = 1.0 / math.sqrt(length)
    cosines = jnp.cos(phases) * factor
    sines = jnp.sin(phases) * factor
    return jnp.concatenate([jnp.stack([cosines, sines], axis=1), jnp.stack([-sines, cosines], axis=1)], axis=0)

def inverse_east_table(points, length, mode_count):
    phases = angles(centered(mode_count), points, length)
    factor = 1.0 / math.sqrt(length)
    return jnp.stack([jnp.cos(phases) * factor, -jnp.sin(phases) * factor], axis=1)

def forward_depth(values, points, frequencies, length):
    phases = angles(frequencies, points, length)
    factor = 1.0 / math.sqrt(length)
    cosines = jnp.cos(phases) * factor
    sines = jnp.sin(phases) * factor
    halfway = values.shape[-1] // 2
    real_in = values[..., :halfway]
    imag_in = values[..., halfway:]
    real_part = jnp.einsum('zcmn,kz->kcmn', real_in, cosines, precision=highest) + jnp.einsum('zcmn,kz->kcmn', imag_in, sines, precision=highest)
    imag_part = jnp.einsum('zcmn,kz->kcmn', imag_in, cosines, precision=highest) - jnp.einsum('zcmn,kz->kcmn', real_in, sines, precision=highest)
    return jnp.concatenate([real_part, imag_part], axis=-1)

def mix_channels(coeffs, weight):
    halfway = coeffs.shape[-1] // 2
    real_in = coeffs[..., :halfway]
    imag_in = coeffs[..., halfway:]
    weight_real = weight[..., :halfway]
    weight_imag = weight[..., halfway:]
    real_part = jnp.einsum('kcmn,kmcon->komn', real_in, weight_real, precision=highest) - jnp.einsum('kcmn,kmcon->komn', imag_in, weight_imag, precision=highest)
    imag_part = jnp.einsum('kcmn,kmcon->komn', imag_in, weight_real, precision=highest) + jnp.einsum('kcmn,kmcon->komn', real_in, weight_imag, precision=highest)
    return jnp.concatenate([real_part, imag_part], axis=-1)

def inverse_depth(values, frequencies, points, length):
    phases = angles(frequencies, points, length)
    factor = 1.0 / math.sqrt(length)
    cosines = jnp.cos(phases) * factor
    sines = jnp.sin(phases) * factor
    halfway = values.shape[-1] // 2
    real_in = values[..., :halfway]
    imag_in = values[..., halfway:]
    real_part = jnp.einsum('komn,kz->zomn', real_in, cosines, precision=highest) - jnp.einsum('komn,kz->zomn', imag_in, sines, precision=highest)
    imag_part = jnp.einsum('komn,kz->zomn', imag_in, cosines, precision=highest) + jnp.einsum('komn,kz->zomn', real_in, sines, precision=highest)
    return jnp.concatenate([real_part, imag_part], axis=-1)

def reference(fields, stiffness, lift_weight, lift_bias, mix_weight, spectral_weight, output_bias):
    fields_now = fields
    for repeat in range(STEPS):
        padded = jnp.pad(fields_now, ((0, 0), (1, 1), (1, 1), (1, 1)), mode='wrap')
        fields_now = step_interior(padded, stiffness)
    filtered = coarsen(fields_now)
    length_depth = filtered.shape[1]
    length_east = filtered.shape[2]
    length_north = filtered.shape[3]
    by_plane = jnp.transpose(filtered, (1, 0, 2, 3))

    def lift_plane(plane_fields):
        lifted_plane = jnp.einsum('fxy,fc->cxy', plane_fields, lift_weight, precision=highest) + lift_bias[:, None, None]
        return jax.nn.gelu(lifted_plane, approximate=True).astype(jnp.bfloat16)
    lifted = lax.map(lift_plane, by_plane)
    east_points = jnp.arange(length_east, dtype=jnp.int32)
    north_points = jnp.arange(length_north, dtype=jnp.int32)
    table_east = forward_east_table(east_points, length_east, MX).astype(jnp.float32)
    table_north = forward_north_table(north_points, length_north, MY)

    def plane_modes(lift_slice):
        east_modes = jnp.einsum('cxy,xpm->cpmy', lift_slice.astype(jnp.float32), table_east, precision=highest)
        return jnp.einsum('cpmy,pyq->cmq', east_modes, table_north, precision=highest)
    north_modes = lax.map(plane_modes, lifted)
    depth_points = jnp.arange(length_depth, dtype=jnp.int32)
    depth_frequencies = jnp.arange(MZ, dtype=jnp.int32)
    coeffs = forward_depth(north_modes, depth_points, depth_frequencies, length_depth)
    mixed_modes = mix_channels(coeffs, spectral_weight)
    back_depth = inverse_depth(mixed_modes, depth_frequencies, depth_points, length_depth)
    back_north_table = inverse_north_table(north_points, length_north, MY)
    back_east_table = inverse_east_table(east_points, length_east, MX)
    mix_wide = mix_weight.astype(jnp.float32)

    def plane_output(paired):
        lift_slice, modes_plane = paired
        back_north = jnp.einsum('omq,qpy->ompy', modes_plane, back_north_table, precision=highest)
        spectral = jnp.einsum('ompy,mpx->oxy', back_north, back_east_table, precision=highest).astype(jnp.bfloat16)
        direct = jnp.einsum('cxy,co->oxy', lift_slice.astype(jnp.float32), mix_wide, precision=highest)
        summed = direct + output_bias[:, None, None] + spectral.astype(jnp.float32)
        return jax.nn.gelu(summed, approximate=True).astype(jnp.bfloat16)
    return lax.map(plane_output, (lifted, back_depth))
```

```python
import math

import functools
import jax
import jax.numpy as jnp
import numpy as np
from jax import lax
from jax.experimental import pallas as pl
from jax.experimental.pallas import tpu as pltpu
from jax.sharding import PartitionSpec as P

STEPS = 3
MX = 32
MY = 64
MZ = 8


courant_half = 0.1
smooth_half = 0.15
mean_flow = (0.3, -0.2, 0.1)
highest = lax.Precision.HIGHEST


def padded_2(block, sides, width):
    for axis, dim in sides:
        count = lax.axis_size(axis)
        forward = [(i, i + 1) for i in range(count - 1)]
        forward.append((count - 1, 0))
        backward = [(target, source) for source, target in forward]
        low = lax.ppermute(
            lax.slice_in_dim(block, block.shape[dim] - width, None, axis=dim), axis, forward
        )
        high = lax.ppermute(lax.slice_in_dim(block, 0, width, axis=dim), axis, backward)
        block = jnp.concatenate([low, block, high], axis=dim)
    return block


def step_interior(padded, stiff_part):
    center = padded[:, 1:-1, 1:-1, 1:-1]
    upper_depth = padded[:, 2:, 1:-1, 1:-1]
    lower_depth = padded[:, :-2, 1:-1, 1:-1]
    upper_east = padded[:, 1:-1, 2:, 1:-1]
    lower_east = padded[:, 1:-1, :-2, 1:-1]
    upper_north = padded[:, 1:-1, 1:-1, 2:]
    lower_north = padded[:, 1:-1, 1:-1, :-2]
    slope_depth = upper_depth - lower_depth
    slope_east = upper_east - lower_east
    slope_north = upper_north - lower_north
    curvature = (
        upper_depth
        + lower_depth
        + upper_east
        + lower_east
        + upper_north
        + lower_north
        - 6.0 * center
    )
    transport = mean_flow[0] * slope_east + mean_flow[1] * slope_north + mean_flow[2] * slope_depth
    diverge = slope_east[1] + slope_north[2] + slope_depth[3]
    coupling = jnp.stack(
        [diverge, slope_east[4], slope_north[4], slope_depth[4], stiff_part * diverge]
    )
    return center - courant_half * (transport + coupling) + smooth_half * curvature


def trim(block, margin):
    return block[margin:-margin, margin:-margin, margin:-margin]


def coarsen(fields_now):
    extent = fields_now.shape
    blocks = fields_now.reshape(extent[0], extent[1], extent[2] // 2, 2, extent[3] // 2, 2)
    return 0.25 * (
        blocks[:, :, :, 0, :, 0]
        + blocks[:, :, :, 1, :, 0]
        + blocks[:, :, :, 0, :, 1]
        + blocks[:, :, :, 1, :, 1]
    )


def angles(frequencies, points, length):
    product = jnp.mod(frequencies[:, None] * points[None, :], length)
    return product.astype(jnp.float32) * (2.0 * math.pi / length)


def centered(number):
    return jnp.arange(number, dtype=jnp.int32) - number // 2


MESH = pl.DeviceIdType.MESH
f32 = jnp.float32
bf16 = jnp.bfloat16


def gelu(v):
    return 0.5 * v * (1.0 + jnp.tanh(math.sqrt(2.0 / math.pi) * (v + 0.044715 * (v * v * v))))


def swapped(v):
    sign = jnp.where(lax.broadcasted_iota(jnp.int32, (v.shape[0], 2 * MY), 1) < MY, 1.0, -1.0)
    parts = [
        pltpu.roll(v[:, i : i + 2 * MY], MY, 1) * sign for i in range(0, v.shape[1], 2 * MY)
    ]
    return jnp.concatenate(parts, axis=1) if len(parts) > 1 else parts[0]


def dot(a, b, dims=((1,), (0,))):
    return lax.dot_general(a, b, (dims, ((), ())), preferred_element_type=f32)


def peers(axis):
    count = lax.axis_size(axis)
    me = lax.axis_index(axis)
    return me, [(d, lax.rem(me + d, count), lax.rem(me + count - d, count)) for d in range(1, count)]


def remote(src, dst, sems, slot, axis, peer):
    return pltpu.make_async_remote_copy(
        src_ref=src,
        dst_ref=dst,
        send_sem=sems[0].at[slot],
        recv_sem=sems[1].at[slot],
        device_id={axis: peer},
        device_id_type=MESH,
    )


def layer_kernel(
    cfg,
    filt, lw, lb, mixk, bias, base_e, base_d, cz, sz, x1, x2, w_hbm,
    out,
    lift, table, p_send, p_recv, p2, r2, q3, r3, c4, r4, rr, ii, mf, r5, r6, s7, r7, wv,
    wsem, s1s, s1r, s2s, s2r, s3s, s3r, s4s, s4r, s5s, s5r, s6s, s6r, s7s, s7r,
):
    G, H, C, CB, KB, OB, KZ, NZL, XL, YL = cfg
    Q = 2 * MY
    gx, gx_peers = peers("gx")
    gy, gy_peers = peers("gy")
    ga = lax.axis_index("ga")
    other = 1 - ga
    weights = pltpu.make_async_copy(w_hbm, wv, wsem)
    weights.start()
    barrier = pltpu.get_barrier_semaphore()
    for axis, group in (("gx", gx_peers), ("gy", gy_peers)):
        for _, peer, _ in group:
            pl.semaphore_signal(barrier, inc=1, device_id={axis: peer}, device_id_type=MESH)
    pl.semaphore_signal(barrier, inc=1, device_id={"ga": other}, device_id_type=MESH)

    e, d = base_e[...], base_d[...]
    for z in range(NZL):
        for k in range(2 * KZ):
            block = e * cz[z, k] + d * sz[z, k]
            table[k // KZ, z * YL : (z + 1) * YL, (k % KZ) * Q : (k % KZ + 1) * Q] = block.astype(bf16)

    def lift_two(pair, carry):
        c = pair * 2
        rows = pl.ds(pl.multiple_of(pair * 2 * XL, 2 * XL), 2 * XL)
        for z in range(NZL):
            halves = []
            for h in range(2):
                v = filt[0, z] * lw[0, c + h]
                for f in range(1, 5):
                    v = v + filt[f, z] * lw[f, c + h]
                halves.append(gelu(v + lb[c + h]))
            lift[rows, z * YL : (z + 1) * YL] = jnp.concatenate(halves, axis=0).astype(bf16)
        return carry

    lax.fori_loop(0, C // 2, lift_two, 0)
    pl.semaphore_wait(barrier, (G - 1) + (H - 1) + 1)

    p_send[...] = dot(lift[...], table[other]).astype(bf16)
    copy = remote(p_send, p_recv, (s1s, s1r), 0, "ga", other)
    copy.start()
    mine = dot(lift[...], table[ga])
    copy.wait()
    total = (mine + p_recv[...].astype(f32)).astype(bf16)
    p2[...] = total.reshape(p2.shape)

    copies = []
    for n, peer, _ in gx_peers:
        copies.append(remote(p2.at[peer], r2.at[gx], (s2s, s2r), n - 1, "gx", peer))
        copies[-1].start()
    r2[gx] = p2[gx]
    for one in copies:
        one.wait()
    v = r2[...].reshape(C * XL, KZ * Q)
    vs = swapped(v.astype(f32)).astype(bf16)
    q3[...] = dot(x1[...], jnp.concatenate([v, vs], axis=0)).astype(bf16).reshape(q3.shape)

    copies = []
    for n, peer, _ in gy_peers:
        copies.append(remote(q3.at[peer], r3.at[n - 1], (s3s, s3r), n - 1, "gy", peer))
        copies[-1].start()
    acc = q3[gy].astype(f32)
    for n, one in enumerate(copies):
        one.wait()
        acc = acc + r3[n].astype(f32)
    c4[...] = acc.astype(bf16)

    copies = []
    for n, peer, _ in gx_peers:
        copies.append(remote(c4, r4.at[gx], (s4s, s4r), n - 1, "gx", peer))
        copies[-1].start()
    r4[gx] = c4[...]
    for one in copies:
        one.wait()
    v = r4[...].reshape(C * KB, KZ * Q).astype(f32)
    low = lax.broadcasted_iota(jnp.int32, (C * KB, Q), 1) < MY
    for k in range(KZ):
        part = v[:, k * Q : (k + 1) * Q]
        turned = pltpu.roll(part, MY, 1)
        rr[k] = jnp.where(low, part, turned)
        ii[k] = jnp.where(low, turned, part)
    weights.wait()

    def mix_one(kx, carry):
        for k in range(KZ):
            lanes = slice(k * Q, (k + 1) * Q)
            a = jnp.zeros((OB, Q), f32)
            b = jnp.zeros((OB, Q), f32)
            for c in range(C):
                w = wv[k, kx, c]
                a = a + w * rr[k, pl.ds(c * KB + kx, 1), :]
                b = b + w * ii[k, pl.ds(c * KB + kx, 1), :]
            mf[kx, :, lanes] = a - swapped(b)
        return carry

    lax.fori_loop(0, KB, mix_one, 0)

    r5[gy] = mf[...].reshape(KB * OB, KZ * Q).astype(bf16)
    copies = []
    for n, peer, _ in gy_peers:
        copies.append(remote(r5.at[gy], r5.at[gy], (s5s, s5r), n - 1, "gy", peer))
        copies[-1].start()
    forwards = [remote(r5.at[gy], r6.at[gy], (s6s, s6r), 0, "ga", other)]
    forwards[0].start()
    for (n, _, source), one in zip(gy_peers, copies):
        one.wait_recv()
        forwards.append(remote(r5.at[source], r6.at[source], (s6s, s6r), n, "ga", other))
        forwards[-1].start()

    def back(v):
        vs = swapped(v.astype(f32)).astype(bf16)
        return dot(x2[...], jnp.concatenate([v, vs], axis=0)).astype(bf16)

    rows = H * KB * OB
    y_mine = back(r5[...].reshape(rows, KZ * Q))
    spec = dot(y_mine, table[ga], ((1,), (1,)))
    for one in copies:
        one.wait_send()
    for one in forwards:
        one.wait()
    y_other = back(r6[...].reshape(rows, KZ * Q))
    spec = spec + dot(y_other, table[other], ((1,), (1,)))
    s7[...] = spec.astype(bf16).reshape(s7.shape)

    copies = []
    for n, peer, _ in gx_peers:
        copies.append(remote(s7.at[peer], r7.at[gx], (s7s, s7r), n - 1, "gx", peer))
        copies[-1].start()
    r7[gx] = s7[gx]
    direct = dot(mixk[...], lift[...]) + bias[...]
    for one in copies:
        one.wait()
    for z in range(NZL):
        lanes = slice(z * YL, (z + 1) * YL)
        both = direct[:, lanes] + r7[:, :, lanes].reshape(C * XL, YL).astype(f32)
        out[z] = gelu(both).astype(bf16).reshape(C, XL, YL)


def east_tables(G, H, XL, C):
    CB, KB, OB = C // G, MX // H, C // G
    length = G * XL
    k = np.arange(MX) - MX // 2
    ang = 2.0 * np.pi * ((k[:, None] * np.arange(length)[None, :]) % length) / length
    scale = 1.0 / math.sqrt(length)
    cos, sin = np.cos(ang) * scale, np.sin(ang) * scale
    cos[np.abs(cos) < 1e-12] = 0.0
    sin[np.abs(sin) < 1e-12] = 0.0

    def forward(t):
        t = t.reshape(H, KB, G, XL)
        full = np.einsum("hkgx,cd->hckgdx", t, np.eye(CB))
        return full.reshape(H * CB * KB, G * CB * XL)

    def inverse(t):
        t = t.reshape(H, KB, G, XL)
        full = np.einsum("hkgx,op->goxhkp", t, np.eye(OB))
        return full.reshape(G * OB * XL, H * KB * OB)

    x1 = np.concatenate([forward(cos), forward(sin)], axis=1)
    x2 = np.concatenate([inverse(cos), -inverse(sin)], axis=1)
    return jnp.asarray(x1, bf16), jnp.asarray(x2, bf16)


def shards(fields, stiffness, lift_weight, lift_bias, mix_weight, spectral_weight, output_bias):
    G, H, A = (lax.axis_size(n) for n in ("gx", "gy", "ga"))
    stacked = jnp.concatenate([fields, stiffness[None]], axis=0)
    padded = padded_2(stacked, (("gx", 2), ("gy", 3), ("ga", 1)), STEPS)
    fields_now = padded[:5]
    for repeat in range(STEPS):
        fields_now = step_interior(fields_now, trim(padded[5], repeat + 1))
    filtered = coarsen(fields_now)
    _, NZL, XL, YL = filtered.shape
    C = lift_weight.shape[1]
    CB, KB, OB, KZ, Q = C // G, MX // H, C // G, MZ // A, 2 * MY
    length_z, length_y = NZL * A, YL * H
    y_points = lax.axis_index("gy") * YL + jnp.arange(YL, dtype=jnp.int32)
    u = angles(centered(MY), y_points, length_y).T
    scale = 1.0 / math.sqrt(length_y * length_z)
    cu, su = jnp.cos(u) * scale, jnp.sin(u) * scale
    base_e = jnp.concatenate([cu, -su], axis=1)
    base_d = jnp.concatenate([-su, -cu], axis=1)
    z_points = lax.axis_index("ga") * NZL + jnp.arange(NZL, dtype=jnp.int32)
    v = angles(jnp.arange(MZ, dtype=jnp.int32), z_points, length_z).T
    x1, x2 = east_tables(G, H, XL, C)
    mixk = jnp.kron(mix_weight.T, jnp.eye(XL, dtype=bf16))
    bias = jnp.repeat(output_bias, XL)[:, None]
    cfg = (G, H, C, CB, KB, OB, KZ, NZL, XL, YL)
    vmem = pl.BlockSpec(memory_space=pltpu.VMEM)
    smem = pl.BlockSpec(memory_space=pltpu.SMEM)
    hbm = pl.BlockSpec(memory_space=pl.ANY)
    L = KZ * Q
    dma = pltpu.SemaphoreType.DMA
    V = pltpu.VMEM
    return pl.pallas_call(
        functools.partial(layer_kernel, cfg),
        out_shape=jax.ShapeDtypeStruct((NZL, C, XL, YL), bf16),
        in_specs=[vmem, smem, smem, vmem, vmem, vmem, vmem, smem, smem, vmem, vmem, hbm],
        out_specs=vmem,
        scratch_shapes=[
            V((C * XL, NZL * YL), bf16),
            V((A, NZL * YL, L), bf16),
            V((C * XL, L), bf16),
            V((C * XL, L), bf16),
            V((G, CB * XL, L), bf16),
            V((G, CB * XL, L), bf16),
            V((H, CB * KB, L), bf16),
            V((H - 1, CB * KB, L), bf16),
            V((CB * KB, L), bf16),
            V((G, CB * KB, L), bf16),
            V((KZ, C * KB, Q), f32),
            V((KZ, C * KB, Q), f32),
            V((KB, OB, L), f32),
            V((H, KB * OB, L), bf16),
            V((H, KB * OB, L), bf16),
            V((G, OB * XL, NZL * YL), bf16),
            V((G, OB * XL, NZL * YL), bf16),
            V(spectral_weight.shape, f32),
            dma,
            dma((1,)), dma((1,)),
            dma((G - 1,)), dma((G - 1,)),
            dma((H - 1,)), dma((H - 1,)),
            dma((G - 1,)), dma((G - 1,)),
            dma((H - 1,)), dma((H - 1,)),
            dma((H,)), dma((H,)),
            dma((G - 1,)), dma((G - 1,)),
        ],
        compiler_params=pltpu.CompilerParams(collective_id=0, has_side_effects=True, vmem_limit_bytes=48 * 2**20),
    )(
        filtered, lift_weight, lift_bias, mixk, bias, base_e, base_d,
        jnp.cos(v), jnp.sin(v), x1, x2, spectral_weight,
    )


def solution(mesh):
    placed = (
        P(None, "ga", "gx", "gy"),
        P("ga", "gx", "gy"),
        P(),
        P(),
        P(),
        P("ga", "gy", None, "gx", None),
        P(),
    )
    return jax.shard_map(
        shards, mesh=mesh, in_specs=placed, out_specs=P("ga", None, "gx", "gy"), check_vma=False
    )
```

```python
import math

import functools
import jax
import jax.numpy as jnp
import numpy as np
from jax import lax
from jax.experimental import pallas as pl
from jax.experimental.pallas import tpu as pltpu
from jax.sharding import PartitionSpec as P

STEPS = 3
MX = 32
MY = 64
MZ = 8


courant_half = 0.1
smooth_half = 0.15
mean_flow = (0.3, -0.2, 0.1)
highest = lax.Precision.HIGHEST


MESH = pl.DeviceIdType.MESH
f32 = jnp.float32
bf16 = jnp.bfloat16


def gelu(v):
    return 0.5 * v * (1.0 + jnp.tanh(math.sqrt(2.0 / math.pi) * (v + 0.044715 * (v * v * v))))


def swapped(v):
    sign = jnp.where(lax.broadcasted_iota(jnp.int32, (v.shape[0], 2 * MY), 1) < MY, 1.0, -1.0)
    parts = [
        pltpu.roll(v[:, i : i + 2 * MY], MY, 1) * sign for i in range(0, v.shape[1], 2 * MY)
    ]
    return jnp.concatenate(parts, axis=1) if len(parts) > 1 else parts[0]


def dot(a, b, dims=((1,), (0,))):
    return lax.dot_general(a, b, (dims, ((), ())), preferred_element_type=f32)


def peers(axis):
    count = lax.axis_size(axis)
    me = lax.axis_index(axis)
    return me, [(d, lax.rem(me + d, count), lax.rem(me + count - d, count)) for d in range(1, count)]


def remote(src, dst, sems, slot, axis, peer):
    return pltpu.make_async_remote_copy(
        src_ref=src,
        dst_ref=dst,
        send_sem=sems[0].at[slot],
        recv_sem=sems[1].at[slot],
        device_id={axis: peer},
        device_id_type=MESH,
    )


def stencil_step(state, target, stiff, xr, yr, dims):
    NZ, NX, NY = dims
    eye = lax.broadcasted_iota(jnp.int32, (NZ * NX, NZ * NX), 0) == lax.broadcasted_iota(
        jnp.int32, (NZ * NX, NZ * NX), 1
    )
    columns = [
        [
            jnp.sum(
                jnp.where(eye, jnp.broadcast_to(yr[side, f : f + 1, :], eye.shape), 0.0),
                axis=1,
                keepdims=True,
            )
            for f in range(5)
        ]
        for side in range(2)
    ]
    row = lax.broadcasted_iota(jnp.int32, (NX, NY), 0)
    lane = lax.broadcasted_iota(jnp.int32, (NX, NY), 1)
    a, b = courant_half, smooth_half
    for z in range(NZ):
        near = []
        for f in range(5):
            c = state[f, z + 1]
            span = slice(z * NX, (z + 1) * NX)
            xl = jnp.where(row == 0, xr[0, f, z : z + 1, :], pltpu.roll(c, 1, 0))
            xu = jnp.where(row == NX - 1, xr[1, f, z : z + 1, :], pltpu.roll(c, NX - 1, 0))
            yl = jnp.where(lane == 0, columns[0][f][span], pltpu.roll(c, 1, 1))
            yu = jnp.where(lane == NY - 1, columns[1][f][span], pltpu.roll(c, NY - 1, 1))
            near.append((c, xl, xu, yl, yu, state[f, z], state[f, z + 2]))
        diverge = (
            (near[1][2] - near[1][1]) + (near[2][4] - near[2][3]) + (near[3][6] - near[3][5])
        )
        p = near[4]
        coupling = (diverge, p[2] - p[1], p[4] - p[3], p[6] - p[5], stiff[z] * diverge)
        for f in range(5):
            c, xl, xu, yl, yu, zl, zu = near[f]
            target[f, z + 1] = (
                (1.0 - 6.0 * b) * c
                + (b + a * mean_flow[0]) * xl
                + (b - a * mean_flow[0]) * xu
                + (b + a * mean_flow[1]) * yl
                + (b - a * mean_flow[1]) * yu
                + (b + a * mean_flow[2]) * zl
                + (b - a * mean_flow[2]) * zu
                - a * coupling[f]
            )


def layer_kernel(
    cfg,
    lw, lb, mix, bias_row, cz, sz, fields_hbm, stiff_hbm, ed_hbm, x1_hbm, x2_hbm, w_hbm,
    out,
    state, stiff, xs, xr, ys, yr, pairs, filt, ed, x1, x2,
    lift, table, p_send, p_recv, p2, r2, q3, r3, c4, r4, rr, ii, mf, r5, r6, s7, r7, wv,
    local, hs, hr, s1s, s1r, s2s, s2r, s3s, s3r, s4s, s4r, s5s, s5r, s6s, s6r, s7s, s7r,
):
    G, H, A, C, CB, KB, OB, KZ, NZL, XL, YL = cfg
    Q = 2 * MY
    NX, NY = 2 * XL, 2 * YL
    gx, gx_peers = peers("gx")
    gy, gy_peers = peers("gy")
    ga = lax.axis_index("ga")
    other = lax.rem(ga + 1, A)
    barrier = pltpu.get_barrier_semaphore()
    for axis, group in (("gx", gx_peers), ("gy", gy_peers)):
        for _, peer, _ in group:
            pl.semaphore_signal(barrier, inc=1, device_id={axis: peer}, device_id_type=MESH)
    pl.semaphore_signal(barrier, inc=1, device_id={"ga": other}, device_id_type=MESH)
    loads = [
        pltpu.make_async_copy(source, target, local.at[n])
        for n, (source, target) in enumerate(
            (
                (fields_hbm, state.at[0, :, pl.ds(1, NZL)]),
                (stiff_hbm, stiff),
                (ed_hbm.at[gy], ed),
                (x1_hbm, x1),
                (x2_hbm, x2),
                (w_hbm, wv),
            )
        )
    ]
    for load in loads:
        load.start()

    def build_table():
        loads[2].wait()
        e, d = ed[0], ed[1]
        for z in range(NZL):
            for k in range(2 * KZ):
                at = ga * NZL + z
                block = e * cz[at, k] + d * sz[at, k]
                table[k // KZ, z * YL : (z + 1) * YL, (k % KZ) * Q : (k % KZ + 1) * Q] = block.astype(bf16)

    loads[0].wait()
    eye = lax.broadcasted_iota(jnp.int32, (NZL * NX, NZL * NX), 0) == lax.broadcasted_iota(
        jnp.int32, (NZL * NX, NZL * NX), 1
    )
    for t in range(STEPS):
        now = state.at[t]
        for side, (edge_x, edge_y) in enumerate(((NX - 1, NY - 1), (0, 0))):
            for f in range(5):
                for z in range(NZL):
                    xs[side, f, z : z + 1, :] = now[f, z + 1, edge_x : edge_x + 1, :]
                column = now[f, 1 : NZL + 1, :, edge_y : edge_y + 1].reshape(NZL * NX, 1)
                ys[side, f : f + 1, :] = jnp.sum(
                    jnp.where(eye, jnp.broadcast_to(column, eye.shape), 0.0), axis=0, keepdims=True
                )
        if t == 0:
            pl.semaphore_wait(barrier, (G - 1) + (H - 1) + 1)
        copies = []
        for side in range(2):
            shift = 1 if side == 0 else -1
            tx, ty, ta = (
                lax.rem(lax.axis_index(n) + lax.axis_size(n) + shift, lax.axis_size(n))
                for n in ("gx", "gy", "ga")
            )
            sems = (hs.at[t], hr.at[t])
            copies.append(remote(ys.at[side], yr.at[t, side], sems, side, "gy", ty))
            copies.append(remote(xs.at[side], xr.at[t, side], sems, 2 + side, "gx", tx))
            plane, halo = (NZL, 0) if side == 0 else (1, NZL + 1)
            copies.append(remote(now.at[:, plane], now.at[:, halo], sems, 4 + side, "ga", ta))
        for one in copies:
            one.start()
        if t == 0:
            build_table()
            loads[1].wait()
        for one in copies:
            one.wait()
        stencil_step(now, state.at[t + 1], stiff, xr.at[t], yr.at[t], (NZL, NX, NY))

    both = lax.broadcasted_iota(jnp.int32, (NY, YL), 0) // 2 == lax.broadcasted_iota(
        jnp.int32, (NY, YL), 1
    )
    both = jnp.where(both, 1.0, 0.0)
    for f in range(5):
        pairs[f] = lax.dot_general(
            state[STEPS, f, 1 : NZL + 1].reshape(NZL * NX, NY),
            both,
            (((1,), (0,)), ((), ())),
            precision=highest,
            preferred_element_type=f32,
        )
        for z in range(NZL):
            filt[f, z] = 0.25 * (
                pairs[f, pl.ds(z * NX, XL, stride=2), :] + pairs[f, pl.ds(z * NX + 1, XL, stride=2), :]
            )

    spread = jnp.where(
        lax.broadcasted_iota(jnp.int32, (C * XL, C), 0) // XL
        == lax.broadcasted_iota(jnp.int32, (C * XL, C), 1),
        1.0,
        0.0,
    )
    bias = jnp.sum(spread * bias_row[...], axis=1, keepdims=True)
    wide = dot(spread.astype(bf16), mix[...], ((1,), (1,))).astype(bf16)
    wide = dot(wide, spread.astype(bf16), ((1,), (1,)))
    same = lax.rem(lax.broadcasted_iota(jnp.int32, wide.shape, 0), XL) == lax.rem(
        lax.broadcasted_iota(jnp.int32, wide.shape, 1), XL
    )
    mixk = jnp.where(same, wide, 0.0).astype(bf16)

    def lift_two(pair, carry):
        c = pair * 2
        rows = pl.ds(pl.multiple_of(pair * 2 * XL, 2 * XL), 2 * XL)
        for z in range(NZL):
            halves = []
            for h in range(2):
                v = filt[0, z] * lw[0, c + h]
                for f in range(1, 5):
                    v = v + filt[f, z] * lw[f, c + h]
                halves.append(gelu(v + lb[c + h]))
            lift[rows, z * YL : (z + 1) * YL] = jnp.concatenate(halves, axis=0).astype(bf16)
        return carry

    lax.fori_loop(0, C // 2, lift_two, 0)

    p_send[...] = dot(lift[...], table[other]).astype(bf16)
    copy = remote(p_send, p_recv, (s1s, s1r), 0, "ga", other)
    copy.start()
    mine = dot(lift[...], table[ga])
    copy.wait()
    total = (mine + p_recv[...].astype(f32)).astype(bf16)
    p2[...] = total.reshape(p2.shape)

    copies = []
    for n, peer, _ in gx_peers:
        copies.append(remote(p2.at[peer], r2.at[gx], (s2s, s2r), n - 1, "gx", peer))
        copies[-1].start()
    r2[gx] = p2[gx]
    for one in copies:
        one.wait()
    loads[3].wait()
    v = r2[...].reshape(C * XL, KZ * Q)
    vs = swapped(v.astype(f32)).astype(bf16)
    q3[...] = dot(x1[...], jnp.concatenate([v, vs], axis=0)).astype(bf16).reshape(q3.shape)

    copies = []
    for n, peer, _ in gy_peers:
        copies.append(remote(q3.at[peer], r3.at[n - 1], (s3s, s3r), n - 1, "gy", peer))
        copies[-1].start()
    acc = q3[gy].astype(f32)
    for n, one in enumerate(copies):
        one.wait()
        acc = acc + r3[n].astype(f32)
    c4[...] = acc.astype(bf16)

    copies = []
    for n, peer, _ in gx_peers:
        copies.append(remote(c4, r4.at[gx], (s4s, s4r), n - 1, "gx", peer))
        copies[-1].start()
    r4[gx] = c4[...]
    for one in copies:
        one.wait()
    v = r4[...].reshape(C * KB, KZ * Q).astype(f32)
    low = lax.broadcasted_iota(jnp.int32, (C * KB, Q), 1) < MY
    for k in range(KZ):
        part = v[:, k * Q : (k + 1) * Q]
        turned = pltpu.roll(part, MY, 1)
        rr[k] = jnp.where(low, part, turned)
        ii[k] = jnp.where(low, turned, part)
    loads[5].wait()

    def mix_one(kx, carry):
        for k in range(KZ):
            lanes = slice(k * Q, (k + 1) * Q)
            a = jnp.zeros((OB, Q), f32)
            b = jnp.zeros((OB, Q), f32)
            for c in range(C):
                w = wv[k, kx, c]
                a = a + w * rr[k, pl.ds(c * KB + kx, 1), :]
                b = b + w * ii[k, pl.ds(c * KB + kx, 1), :]
            mf[kx, :, lanes] = a - swapped(b)
        return carry

    lax.fori_loop(0, KB, mix_one, 0)

    r5[gy] = mf[...].reshape(KB * OB, KZ * Q).astype(bf16)
    copies = []
    for n, peer, _ in gy_peers:
        copies.append(remote(r5.at[gy], r5.at[gy], (s5s, s5r), n - 1, "gy", peer))
        copies[-1].start()
    forwards = [remote(r5.at[gy], r6.at[gy], (s6s, s6r), 0, "ga", other)]
    forwards[0].start()
    for (n, _, source), one in zip(gy_peers, copies):
        one.wait_recv()
        forwards.append(remote(r5.at[source], r6.at[source], (s6s, s6r), n, "ga", other))
        forwards[-1].start()

    loads[4].wait()

    def back(v):
        vs = swapped(v.astype(f32)).astype(bf16)
        return dot(x2[...], jnp.concatenate([v, vs], axis=0)).astype(bf16)

    rows = H * KB * OB
    y_mine = back(r5[...].reshape(rows, KZ * Q))
    spec = dot(y_mine, table[ga], ((1,), (1,)))
    for one in copies:
        one.wait_send()
    for one in forwards:
        one.wait()
    y_other = back(r6[...].reshape(rows, KZ * Q))
    spec = spec + dot(y_other, table[other], ((1,), (1,)))
    s7[...] = spec.astype(bf16).reshape(s7.shape)

    copies = []
    for n, peer, _ in gx_peers:
        copies.append(remote(s7.at[peer], r7.at[gx], (s7s, s7r), n - 1, "gx", peer))
        copies[-1].start()
    r7[gx] = s7[gx]
    direct = dot(mixk, lift[...]) + bias
    for one in copies:
        one.wait()
    for z in range(NZL):
        lanes = slice(z * YL, (z + 1) * YL)
        both = direct[:, lanes] + r7[:, :, lanes].reshape(C * XL, YL).astype(f32)
        out[z] = gelu(both).astype(bf16).reshape(C, XL, YL)


def east_tables(G, H, XL, C):
    CB, KB, OB = C // G, MX // H, C // G
    length = G * XL
    k = np.arange(MX) - MX // 2
    ang = 2.0 * np.pi * ((k[:, None] * np.arange(length)[None, :]) % length) / length
    scale = 1.0 / math.sqrt(length)
    cos, sin = np.cos(ang) * scale, np.sin(ang) * scale
    cos[np.abs(cos) < 1e-12] = 0.0
    sin[np.abs(sin) < 1e-12] = 0.0

    def forward(t):
        t = t.reshape(H, KB, G, XL)
        full = np.einsum("hkgx,cd->hckgdx", t, np.eye(CB))
        return full.reshape(H * CB * KB, G * CB * XL)

    def inverse(t):
        t = t.reshape(H, KB, G, XL)
        full = np.einsum("hkgx,op->goxhkp", t, np.eye(OB))
        return full.reshape(G * OB * XL, H * KB * OB)

    x1 = np.concatenate([forward(cos), forward(sin)], axis=1)
    x2 = np.concatenate([inverse(cos), -inverse(sin)], axis=1)
    return jnp.asarray(x1, bf16), jnp.asarray(x2, bf16)


def north_tables(H, YL, NZ):
    length = H * YL
    n = np.arange(MY) - MY // 2
    u = 2.0 * np.pi * ((np.arange(length)[:, None] * n[None, :]) % length) / length
    scale = 1.0 / math.sqrt(length * NZ)
    cu, su = np.cos(u) * scale, np.sin(u) * scale
    both = np.stack([np.concatenate([cu, -su], axis=1), np.concatenate([-su, -cu], axis=1)])
    return jnp.asarray(both.reshape(2, H, YL, 2 * MY).transpose(1, 0, 2, 3), f32)


def shards(fields, stiffness, lift_weight, lift_bias, mix_weight, spectral_weight, output_bias):
    G, H, A = (lax.axis_size(n) for n in ("gx", "gy", "ga"))
    _, NZL, NX, NY = fields.shape
    XL, YL = NX // 2, NY // 2
    C = lift_weight.shape[1]
    CB, KB, OB, KZ, Q = C // G, MX // H, C // G, MZ // A, 2 * MY
    NZ = NZL * A
    v = 2.0 * np.pi * ((np.arange(NZ)[:, None] * np.arange(MZ)[None, :]) % NZ) / NZ
    x1, x2 = east_tables(G, H, XL, C)
    ed = north_tables(H, YL, NZ)
    cfg = (G, H, A, C, CB, KB, OB, KZ, NZL, XL, YL)
    vmem = pl.BlockSpec(memory_space=pltpu.VMEM)
    smem = pl.BlockSpec(memory_space=pltpu.SMEM)
    hbm = pl.BlockSpec(memory_space=pl.ANY)
    L = KZ * Q
    dma = pltpu.SemaphoreType.DMA
    V = pltpu.VMEM
    return pl.pallas_call(
        functools.partial(layer_kernel, cfg),
        out_shape=jax.ShapeDtypeStruct((NZL, C, XL, YL), bf16),
        in_specs=[smem, smem, vmem, vmem, smem, smem, hbm, hbm, hbm, hbm, hbm, hbm],
        out_specs=vmem,
        scratch_shapes=[
            V((STEPS + 1, 5, NZL + 2, NX, NY), f32),
            V((NZL, NX, NY), f32),
            V((2, 5, NZL, NY), f32),
            V((STEPS, 2, 5, NZL, NY), f32),
            V((2, 5, NZL * NX), f32),
            V((STEPS, 2, 5, NZL * NX), f32),
            V((5, NZL * NX, YL), f32),
            V((5, NZL, XL, YL), f32),
            V(ed.shape[1:], f32),
            V(x1.shape, bf16),
            V(x2.shape, bf16),
            V((C * XL, NZL * YL), bf16),
            V((A, NZL * YL, L), bf16),
            V((C * XL, L), bf16),
            V((C * XL, L), bf16),
            V((G, CB * XL, L), bf16),
            V((G, CB * XL, L), bf16),
            V((H, CB * KB, L), bf16),
            V((H - 1, CB * KB, L), bf16),
            V((CB * KB, L), bf16),
            V((G, CB * KB, L), bf16),
            V((KZ, C * KB, Q), f32),
            V((KZ, C * KB, Q), f32),
            V((KB, OB, L), f32),
            V((H, KB * OB, L), bf16),
            V((H, KB * OB, L), bf16),
            V((G, OB * XL, NZL * YL), bf16),
            V((G, OB * XL, NZL * YL), bf16),
            V(spectral_weight.shape, f32),
            dma((6,)),
            dma((STEPS, 6)), dma((STEPS, 6)),
            dma((1,)), dma((1,)),
            dma((G - 1,)), dma((G - 1,)),
            dma((H - 1,)), dma((H - 1,)),
            dma((G - 1,)), dma((G - 1,)),
            dma((H - 1,)), dma((H - 1,)),
            dma((H,)), dma((H,)),
            dma((G - 1,)), dma((G - 1,)),
        ],
        compiler_params=pltpu.CompilerParams(collective_id=0, has_side_effects=True, vmem_limit_bytes=48 * 2**20),
    )(
        lift_weight, lift_bias, mix_weight, output_bias[None, :],
        jnp.asarray(np.cos(v), f32), jnp.asarray(np.sin(v), f32),
        fields, stiffness, ed, x1, x2, spectral_weight,
    )


def solution(mesh):
    placed = (
        P(None, "ga", "gx", "gy"),
        P("ga", "gx", "gy"),
        P(),
        P(),
        P(),
        P("ga", "gy", None, "gx", None),
        P(),
    )
    return jax.shard_map(
        shards, mesh=mesh, in_specs=placed, out_specs=P("ga", None, "gx", "gy"), check_vma=False
    )
```

```python
import math

import functools
import jax
import jax.numpy as jnp
import numpy as np
from jax import lax
from jax.experimental import pallas as pl
from jax.experimental.pallas import tpu as pltpu
from jax.sharding import PartitionSpec as P

STEPS = 3
MX = 32
MY = 64
MZ = 8
MODE_CHUNKS = 2
DEPTH_CHUNKS = 4


courant_half = 0.1
smooth_half = 0.15
mean_flow = (0.3, -0.2, 0.1)
highest = lax.Precision.HIGHEST


MESH = pl.DeviceIdType.MESH
f32 = jnp.float32
bf16 = jnp.bfloat16


def gelu(v):
    return 0.5 * v * (1.0 + jnp.tanh(math.sqrt(2.0 / math.pi) * (v + 0.044715 * (v * v * v))))


def swapped(v):
    sign = jnp.where(lax.broadcasted_iota(jnp.int32, (v.shape[0], 2 * MY), 1) < MY, 1.0, -1.0)
    parts = [
        pltpu.roll(v[:, i : i + 2 * MY], MY, 1) * sign for i in range(0, v.shape[1], 2 * MY)
    ]
    return jnp.concatenate(parts, axis=1) if len(parts) > 1 else parts[0]


def dot(a, b, dims=((1,), (0,))):
    return lax.dot_general(a, b, (dims, ((), ())), preferred_element_type=f32)


def peers(axis):
    count = lax.axis_size(axis)
    me = lax.axis_index(axis)
    return me, [(d, lax.rem(me + d, count), lax.rem(me + count - d, count)) for d in range(1, count)]


def remote(src, dst, sems, slot, axis, peer):
    return pltpu.make_async_remote_copy(
        src_ref=src,
        dst_ref=dst,
        send_sem=sems[0].at[slot],
        recv_sem=sems[1].at[slot],
        device_id={axis: peer},
        device_id_type=MESH,
    )


def stencil_step(state, target, stiff, xr, yr, dims):
    NZ, NX, NY = dims
    eye = lax.broadcasted_iota(jnp.int32, (NZ * NX, NZ * NX), 0) == lax.broadcasted_iota(
        jnp.int32, (NZ * NX, NZ * NX), 1
    )
    columns = [
        [
            jnp.sum(
                jnp.where(eye, jnp.broadcast_to(yr[side, f : f + 1, :], eye.shape), 0.0),
                axis=1,
                keepdims=True,
            )
            for f in range(5)
        ]
        for side in range(2)
    ]
    row = lax.broadcasted_iota(jnp.int32, (NX, NY), 0)
    lane = lax.broadcasted_iota(jnp.int32, (NX, NY), 1)
    a, b = courant_half, smooth_half
    for z in range(NZ):
        near = []
        for f in range(5):
            c = state[f, z + 1]
            span = slice(z * NX, (z + 1) * NX)
            xl = jnp.where(row == 0, xr[0, f, z : z + 1, :], pltpu.roll(c, 1, 0))
            xu = jnp.where(row == NX - 1, xr[1, f, z : z + 1, :], pltpu.roll(c, NX - 1, 0))
            yl = jnp.where(lane == 0, columns[0][f][span], pltpu.roll(c, 1, 1))
            yu = jnp.where(lane == NY - 1, columns[1][f][span], pltpu.roll(c, NY - 1, 1))
            near.append((c, xl, xu, yl, yu, state[f, z], state[f, z + 2]))
        diverge = (
            (near[1][2] - near[1][1]) + (near[2][4] - near[2][3]) + (near[3][6] - near[3][5])
        )
        p = near[4]
        coupling = (diverge, p[2] - p[1], p[4] - p[3], p[6] - p[5], stiff[z] * diverge)
        for f in range(5):
            c, xl, xu, yl, yu, zl, zu = near[f]
            target[f, z + 1] = (
                (1.0 - 6.0 * b) * c
                + (b + a * mean_flow[0]) * xl
                + (b - a * mean_flow[0]) * xu
                + (b + a * mean_flow[1]) * yl
                + (b - a * mean_flow[1]) * yu
                + (b + a * mean_flow[2]) * zl
                + (b - a * mean_flow[2]) * zu
                - a * coupling[f]
            )


def layer_kernel(
    cfg,
    fields_hbm, stiff_hbm, ed_hbm, x1_hbm, x2_hbm, w_hbm, lw_hbm, lb_hbm, mix_hbm, bias_hbm,
    out,
    state, stiff, xs, xr, ys, yr, pairs, filt, ed, x1, x2, wv, lw, lb, mix, bias_row, wide_lift,
    lift, table, p_send, p_recv, p2, r2, q3, r3, c4, r4, rr, ii, mf, r5, r6, s7, r7,
    local, hs, hr, s1s, s1r, s2s, s2r, s3s, s3r, s4s, s4r, s5s, s5r, s6s, s6r, s7s, s7r,
):
    G, H, A, C, CB, KB, OB, KZ, NZL, XL, YL = cfg
    Q = 2 * MY
    NX, NY = 2 * XL, 2 * YL
    gx, gx_peers = peers("gx")
    gy, gy_peers = peers("gy")
    ga = lax.axis_index("ga")
    other = lax.rem(ga + 1, A)
    barrier = pltpu.get_barrier_semaphore()
    for axis, group in (("gx", gx_peers), ("gy", gy_peers)):
        for _, peer, _ in group:
            pl.semaphore_signal(barrier, inc=1, device_id={axis: peer}, device_id_type=MESH)
    pl.semaphore_signal(barrier, inc=1, device_id={"ga": other}, device_id_type=MESH)
    loads = [
        pltpu.make_async_copy(source, target, local.at[n])
        for n, (source, target) in enumerate(
            (
                (fields_hbm, state.at[0, :, pl.ds(1, NZL)]),
                (stiff_hbm, stiff),
                (ed_hbm.at[gy], ed),
                (x1_hbm, x1),
                (x2_hbm, x2),
                (w_hbm, wv),
                (lw_hbm, lw),
                (lb_hbm, lb),
                (mix_hbm, mix),
                (bias_hbm, bias_row),
            )
        )
    ]
    for load in loads:
        load.start()

    NCH, NZC = MODE_CHUNKS, DEPTH_CHUNKS
    KC = KZ // NCH
    W = KC * Q
    ZC = NZL // NZC
    NZ = NZL * A

    def own(values):
        picked = jnp.float32(values[0])
        for n in range(1, A):
            picked = jnp.where(ga == n, jnp.float32(values[n]), picked)
        return picked

    def build_table():
        loads[2].wait()
        e, d = ed[0], ed[1]
        for z in range(NZL):
            for k in range(A * KZ):
                v = [2.0 * math.pi * ((k * (n * NZL + z)) % NZ) / NZ for n in range(A)]
                block = e * own([math.cos(x) for x in v]) + d * own([math.sin(x) for x in v])
                table[k // KC, z * YL : (z + 1) * YL, (k % KC) * Q : (k % KC + 1) * Q] = block.astype(bf16)

    spread = jnp.where(
        lax.broadcasted_iota(jnp.int32, (C * XL, C), 0) // XL
        == lax.broadcasted_iota(jnp.int32, (C * XL, C), 1),
        1.0,
        0.0,
    )

    def tall(values):
        return jnp.sum(spread * values, axis=1, keepdims=True)

    def build_lift():
        for n in (6, 7):
            loads[n].wait()
        for f in range(6):
            values = lw[f : f + 1, :] if f < 5 else lb[...]
            wide_lift[f] = jnp.broadcast_to(tall(values), (C * XL, YL))

    loads[0].wait()
    eye = lax.broadcasted_iota(jnp.int32, (NZL * NX, NZL * NX), 0) == lax.broadcasted_iota(
        jnp.int32, (NZL * NX, NZL * NX), 1
    )
    for t in range(STEPS):
        now = state.at[t]
        for side, (edge_x, edge_y) in enumerate(((NX - 1, NY - 1), (0, 0))):
            for f in range(5):
                for z in range(NZL):
                    xs[side, f, z : z + 1, :] = now[f, z + 1, edge_x : edge_x + 1, :]
                column = now[f, 1 : NZL + 1, :, edge_y : edge_y + 1].reshape(NZL * NX, 1)
                ys[side, f : f + 1, :] = jnp.sum(
                    jnp.where(eye, jnp.broadcast_to(column, eye.shape), 0.0), axis=0, keepdims=True
                )
        if t == 0:
            pl.semaphore_wait(barrier, (G - 1) + (H - 1) + 1)
        copies = []
        for side in range(2):
            shift = 1 if side == 0 else -1
            tx, ty, ta = (
                lax.rem(lax.axis_index(n) + lax.axis_size(n) + shift, lax.axis_size(n))
                for n in ("gx", "gy", "ga")
            )
            sems = (hs.at[t], hr.at[t])
            copies.append(remote(ys.at[side], yr.at[t, side], sems, side, "gy", ty))
            copies.append(remote(xs.at[side], xr.at[t, side], sems, 2 + side, "gx", tx))
            plane, halo = (NZL, 0) if side == 0 else (1, NZL + 1)
            copies.append(remote(now.at[:, plane], now.at[:, halo], sems, 4 + side, "ga", ta))
        for one in copies:
            one.start()
        if t == 0:
            build_table()
            loads[1].wait()
        if t == STEPS - 1:
            build_lift()
        for one in copies:
            one.wait()
        stencil_step(now, state.at[t + 1], stiff, xr.at[t], yr.at[t], (NZL, NX, NY))

    both = lax.broadcasted_iota(jnp.int32, (NY, YL), 0) // 2 == lax.broadcasted_iota(
        jnp.int32, (NY, YL), 1
    )
    both = jnp.where(both, 1.0, 0.0)
    for f in range(5):
        pairs[f] = lax.dot_general(
            state[STEPS, f, 1 : NZL + 1].reshape(NZL * NX, NY),
            both,
            (((1,), (0,)), ((), ())),
            precision=highest,
            preferred_element_type=f32,
        )
        for z in range(NZL):
            filt[f, z] = 0.25 * (
                pairs[f, pl.ds(z * NX, XL, stride=2), :] + pairs[f, pl.ds(z * NX + 1, XL, stride=2), :]
            )

    def lift_two(pair, carry):
        rows = pl.ds(pl.multiple_of(pair * 2 * XL, 2 * XL), 2 * XL)
        weights = [wide_lift[f, rows, :] for f in range(6)]
        for z in range(NZL):
            v = weights[5]
            for f in range(5):
                v = v + jnp.concatenate([filt[f, z], filt[f, z]], axis=0) * weights[f]
            lift[rows, z * YL : (z + 1) * YL] = gelu(v).astype(bf16)
        return carry

    lax.fori_loop(0, C // 2, lift_two, 0)

    stage1 = []
    for h in range(NCH):
        p_send[h] = dot(lift[...], table[other * NCH + h]).astype(bf16)
        stage1.append(remote(p_send.at[h], p_recv.at[h], (s1s, s1r), h, "ga", other))
        stage1[-1].start()

    stage2 = []
    for h in range(NCH):
        mine = dot(lift[...], table[ga * NCH + h])
        stage1[h].wait()
        p2[h] = (mine + p_recv[h].astype(f32)).astype(bf16).reshape(p2.shape[1:])
        group = []
        for n, peer, _ in gx_peers:
            slot = h * (G - 1) + n - 1
            group.append(remote(p2.at[h, peer], r2.at[h, gx], (s2s, s2r), slot, "gx", peer))
            group[-1].start()
        r2[h, gx] = p2[h, gx]
        stage2.append(group)

    loads[3].wait()
    stage3 = []
    for h in range(NCH):
        for one in stage2[h]:
            one.wait()
        v = r2[h].reshape(C * XL, W)
        vs = swapped(v.astype(f32)).astype(bf16)
        q3[h] = dot(x1[...], jnp.concatenate([v, vs], axis=0)).astype(bf16).reshape(q3.shape[1:])
        group = []
        for n, peer, _ in gy_peers:
            slot = h * (H - 1) + n - 1
            group.append(remote(q3.at[h, peer], r3.at[h, n - 1], (s3s, s3r), slot, "gy", peer))
            group[-1].start()
        stage3.append(group)

    stage4 = []
    for h in range(NCH):
        acc = q3[h, gy].astype(f32)
        for n, one in enumerate(stage3[h]):
            one.wait()
            acc = acc + r3[h, n].astype(f32)
        c4[h] = acc.astype(bf16)
        group = []
        for n, peer, _ in gx_peers:
            slot = h * (G - 1) + n - 1
            group.append(remote(c4.at[h], r4.at[h, gx], (s4s, s4r), slot, "gx", peer))
            group[-1].start()
        r4[h, gx] = c4[h]
        stage4.append(group)

    loads[5].wait()
    low = lax.broadcasted_iota(jnp.int32, (C * KB, Q), 1) < MY
    stage5 = []
    stage6 = []
    for h in range(NCH):
        for one in stage4[h]:
            one.wait()
        v = r4[h].reshape(C * KB, W).astype(f32)
        for k in range(KC):
            part = v[:, k * Q : (k + 1) * Q]
            turned = pltpu.roll(part, MY, 1)
            rr[h * KC + k] = jnp.where(low, part, turned)
            ii[h * KC + k] = jnp.where(low, turned, part)

        def mix_one(kx, carry):
            for k in range(KC):
                a = jnp.zeros((OB, Q), f32)
                b = jnp.zeros((OB, Q), f32)
                for c in range(C):
                    w = wv[h * KC + k, kx, c]
                    a = a + w * rr[h * KC + k, pl.ds(c * KB + kx, 1), :]
                    b = b + w * ii[h * KC + k, pl.ds(c * KB + kx, 1), :]
                mf[h, kx, :, k * Q : (k + 1) * Q] = a - swapped(b)
            return carry

        lax.fori_loop(0, KB, mix_one, 0)
        r5[h, gy] = mf[h].reshape(KB * OB, W).astype(bf16)
        group = []
        for n, peer, _ in gy_peers:
            slot = h * (H - 1) + n - 1
            group.append(remote(r5.at[h, gy], r5.at[h, gy], (s5s, s5r), slot, "gy", peer))
            group[-1].start()
        stage5.append(group)
        stage6.append([remote(r5.at[h, gy], r6.at[h, gy], (s6s, s6r), h * H, "ga", other)])
        stage6[h][0].start()

    loads[8].wait()
    loads[9].wait()
    bias = tall(bias_row[...])
    wide = dot(spread.astype(bf16), mix[...], ((1,), (1,))).astype(bf16)
    wide = dot(wide, spread.astype(bf16), ((1,), (1,)))
    same = lax.rem(lax.broadcasted_iota(jnp.int32, wide.shape, 0), XL) == lax.rem(
        lax.broadcasted_iota(jnp.int32, wide.shape, 1), XL
    )
    mixk = jnp.where(same, wide, 0.0).astype(bf16)

    loads[4].wait()
    rows = H * KB * OB

    def back(v):
        v = v.reshape(rows, W)
        vs = swapped(v.astype(f32)).astype(bf16)
        return dot(x2[...], jnp.concatenate([v, vs], axis=0)).astype(bf16)

    modes = []
    for h in range(NCH):
        for (n, _, source), one in zip(gy_peers, stage5[h]):
            one.wait_recv()
            stage6[h].append(
                remote(r5.at[h, source], r6.at[h, source], (s6s, s6r), h * H + n, "ga", other)
            )
            stage6[h][-1].start()
        modes.append((ga * NCH + h, back(r5[h])))
    for h in range(NCH):
        for one in stage5[h]:
            one.wait_send()
        for one in stage6[h]:
            one.wait()
        modes.append((other * NCH + h, back(r6[h])))

    stage7 = []
    for j in range(NZC):
        span = slice(j * ZC * YL, (j + 1) * ZC * YL)
        spec = dot(modes[0][1], table[modes[0][0], span, :], ((1,), (1,)))
        for at, y in modes[1:]:
            spec = spec + dot(y, table[at, span, :], ((1,), (1,)))
        s7[j] = spec.astype(bf16).reshape(s7.shape[1:])
        group = []
        for n, peer, _ in gx_peers:
            slot = j * (G - 1) + n - 1
            group.append(remote(s7.at[j, peer], r7.at[j, gx], (s7s, s7r), slot, "gx", peer))
            group[-1].start()
        r7[j, gx] = s7[j, gx]
        stage7.append(group)
    for j in range(NZC):
        span = slice(j * ZC * YL, (j + 1) * ZC * YL)
        direct = dot(mixk, lift[:, span]) + bias
        for one in stage7[j]:
            one.wait()
        both = gelu(direct + r7[j].reshape(C * XL, ZC * YL).astype(f32)).astype(bf16)
        for z in range(ZC):
            out[j * ZC + z] = both[:, z * YL : (z + 1) * YL].reshape(C, XL, YL)


def east_tables(G, H, XL, C):
    CB, KB, OB = C // G, MX // H, C // G
    length = G * XL
    k = np.arange(MX) - MX // 2
    ang = 2.0 * np.pi * ((k[:, None] * np.arange(length)[None, :]) % length) / length
    scale = 1.0 / math.sqrt(length)
    cos, sin = np.cos(ang) * scale, np.sin(ang) * scale
    cos[np.abs(cos) < 1e-12] = 0.0
    sin[np.abs(sin) < 1e-12] = 0.0

    def forward(t):
        t = t.reshape(H, KB, G, XL)
        full = np.einsum("hkgx,cd->hckgdx", t, np.eye(CB))
        return full.reshape(H * CB * KB, G * CB * XL)

    def inverse(t):
        t = t.reshape(H, KB, G, XL)
        full = np.einsum("hkgx,op->goxhkp", t, np.eye(OB))
        return full.reshape(G * OB * XL, H * KB * OB)

    x1 = np.concatenate([forward(cos), forward(sin)], axis=1)
    x2 = np.concatenate([inverse(cos), -inverse(sin)], axis=1)
    return jnp.asarray(x1, bf16), jnp.asarray(x2, bf16)


def north_tables(H, YL, NZ):
    length = H * YL
    n = np.arange(MY) - MY // 2
    u = 2.0 * np.pi * ((np.arange(length)[:, None] * n[None, :]) % length) / length
    scale = 1.0 / math.sqrt(length * NZ)
    cu, su = np.cos(u) * scale, np.sin(u) * scale
    both = np.stack([np.concatenate([cu, -su], axis=1), np.concatenate([-su, -cu], axis=1)])
    return jnp.asarray(both.reshape(2, H, YL, 2 * MY).transpose(1, 0, 2, 3), f32)


def shards(fields, stiffness, lift_weight, lift_bias, mix_weight, spectral_weight, output_bias):
    G, H, A = (lax.axis_size(n) for n in ("gx", "gy", "ga"))
    _, NZL, NX, NY = fields.shape
    XL, YL = NX // 2, NY // 2
    C = lift_weight.shape[1]
    CB, KB, OB, KZ, Q = C // G, MX // H, C // G, MZ // A, 2 * MY
    NZ = NZL * A
    x1, x2 = east_tables(G, H, XL, C)
    ed = north_tables(H, YL, NZ)
    cfg = (G, H, A, C, CB, KB, OB, KZ, NZL, XL, YL)
    vmem = pl.BlockSpec(memory_space=pltpu.VMEM)
    hbm = pl.BlockSpec(memory_space=pltpu.HBM)
    NCH, NZC = MODE_CHUNKS, DEPTH_CHUNKS
    W = KZ // NCH * Q
    ZW = NZL // NZC * YL
    dma = pltpu.SemaphoreType.DMA
    V = pltpu.VMEM
    return pl.pallas_call(
        functools.partial(layer_kernel, cfg),
        out_shape=jax.ShapeDtypeStruct((NZL, C, XL, YL), bf16),
        in_specs=[hbm] * 10,
        out_specs=vmem,
        scratch_shapes=[
            V((STEPS + 1, 5, NZL + 2, NX, NY), f32),
            V((NZL, NX, NY), f32),
            V((2, 5, NZL, NY), f32),
            V((STEPS, 2, 5, NZL, NY), f32),
            V((2, 5, NZL * NX), f32),
            V((STEPS, 2, 5, NZL * NX), f32),
            V((5, NZL * NX, YL), f32),
            V((5, NZL, XL, YL), f32),
            V(ed.shape[1:], f32),
            V(x1.shape, bf16),
            V(x2.shape, bf16),
            V(spectral_weight.shape, f32),
            V(lift_weight.shape, f32),
            V((1, C), f32),
            V(mix_weight.shape, bf16),
            V((1, C), f32),
            V((6, C * XL, YL), f32),
            V((C * XL, NZL * YL), bf16),
            V((A * NCH, NZL * YL, W), bf16),
            V((NCH, C * XL, W), bf16),
            V((NCH, C * XL, W), bf16),
            V((NCH, G, CB * XL, W), bf16),
            V((NCH, G, CB * XL, W), bf16),
            V((NCH, H, CB * KB, W), bf16),
            V((NCH, H - 1, CB * KB, W), bf16),
            V((NCH, CB * KB, W), bf16),
            V((NCH, G, CB * KB, W), bf16),
            V((KZ, C * KB, Q), f32),
            V((KZ, C * KB, Q), f32),
            V((NCH, KB, OB, W), f32),
            V((NCH, H, KB * OB, W), bf16),
            V((NCH, H, KB * OB, W), bf16),
            V((NZC, G, OB * XL, ZW), bf16),
            V((NZC, G, OB * XL, ZW), bf16),
            dma((10,)),
            dma((STEPS, 6)), dma((STEPS, 6)),
            dma((NCH,)), dma((NCH,)),
            dma((NCH * (G - 1),)), dma((NCH * (G - 1),)),
            dma((NCH * (H - 1),)), dma((NCH * (H - 1),)),
            dma((NCH * (G - 1),)), dma((NCH * (G - 1),)),
            dma((NCH * (H - 1),)), dma((NCH * (H - 1),)),
            dma((NCH * H,)), dma((NCH * H,)),
            dma((NZC * (G - 1),)), dma((NZC * (G - 1),)),
        ],
        compiler_params=pltpu.CompilerParams(collective_id=0, has_side_effects=True, vmem_limit_bytes=48 * 2**20),
    )(
        fields, stiffness, ed, x1, x2, spectral_weight,
        lift_weight, lift_bias[None, :], mix_weight, output_bias[None, :],
    )


def solution(mesh):
    placed = (
        P(None, "ga", "gx", "gy"),
        P("ga", "gx", "gy"),
        P(),
        P(),
        P(),
        P("ga", "gy", None, "gx", None),
        P(),
    )
    return jax.shard_map(
        shards, mesh=mesh, in_specs=placed, out_specs=P("ga", None, "gx", "gy"), check_vma=False
    )
```

```python
import math

import functools
import jax
import jax.numpy as jnp
import numpy as np
from jax import lax
from jax.experimental import pallas as pl
from jax.experimental.pallas import tpu as pltpu
from jax.sharding import PartitionSpec as P

STEPS = 3
MX = 32
MY = 64
MZ = 8
MODE_CHUNKS = 4
DEPTH_CHUNKS = 4


courant_half = 0.1
smooth_half = 0.15
mean_flow = (0.3, -0.2, 0.1)
highest = lax.Precision.HIGHEST


MESH = pl.DeviceIdType.MESH
f32 = jnp.float32
bf16 = jnp.bfloat16


def gelu(v):
    return 0.5 * v * (1.0 + jnp.tanh(math.sqrt(2.0 / math.pi) * (v + 0.044715 * (v * v * v))))


def swapped(v):
    sign = jnp.where(lax.broadcasted_iota(jnp.int32, (v.shape[0], 2 * MY), 1) < MY, 1.0, -1.0)
    parts = [
        pltpu.roll(v[:, i : i + 2 * MY], MY, 1) * sign for i in range(0, v.shape[1], 2 * MY)
    ]
    return jnp.concatenate(parts, axis=1) if len(parts) > 1 else parts[0]


def dot(a, b, dims=((1,), (0,))):
    return lax.dot_general(a, b, (dims, ((), ())), preferred_element_type=f32)


def peers(axis):
    count = lax.axis_size(axis)
    me = lax.axis_index(axis)
    return me, [(d, lax.rem(me + d, count), lax.rem(me + count - d, count)) for d in range(1, count)]


def remote(src, dst, sems, slot, axis, peer):
    return pltpu.make_async_remote_copy(
        src_ref=src,
        dst_ref=dst,
        send_sem=sems[0].at[slot],
        recv_sem=sems[1].at[slot],
        device_id={axis: peer},
        device_id_type=MESH,
    )


def stencil_step(state, target, stiff, xr, yr, dims):
    NZ, NX, NY = dims
    eye = lax.broadcasted_iota(jnp.int32, (NZ * NX, NZ * NX), 0) == lax.broadcasted_iota(
        jnp.int32, (NZ * NX, NZ * NX), 1
    )
    columns = [
        [
            jnp.sum(
                jnp.where(eye, jnp.broadcast_to(yr[side, f : f + 1, :], eye.shape), 0.0),
                axis=1,
                keepdims=True,
            )
            for f in range(5)
        ]
        for side in range(2)
    ]
    row = lax.broadcasted_iota(jnp.int32, (NX, NY), 0)
    lane = lax.broadcasted_iota(jnp.int32, (NX, NY), 1)
    a, b = courant_half, smooth_half
    for z in range(NZ):
        near = []
        for f in range(5):
            c = state[f, z + 1]
            span = slice(z * NX, (z + 1) * NX)
            xl = jnp.where(row == 0, xr[0, f, z : z + 1, :], pltpu.roll(c, 1, 0))
            xu = jnp.where(row == NX - 1, xr[1, f, z : z + 1, :], pltpu.roll(c, NX - 1, 0))
            yl = jnp.where(lane == 0, columns[0][f][span], pltpu.roll(c, 1, 1))
            yu = jnp.where(lane == NY - 1, columns[1][f][span], pltpu.roll(c, NY - 1, 1))
            near.append((c, xl, xu, yl, yu, state[f, z], state[f, z + 2]))
        diverge = (
            (near[1][2] - near[1][1]) + (near[2][4] - near[2][3]) + (near[3][6] - near[3][5])
        )
        p = near[4]
        coupling = (diverge, p[2] - p[1], p[4] - p[3], p[6] - p[5], stiff[z] * diverge)
        for f in range(5):
            c, xl, xu, yl, yu, zl, zu = near[f]
            target[f, z + 1] = (
                (1.0 - 6.0 * b) * c
                + (b + a * mean_flow[0]) * xl
                + (b - a * mean_flow[0]) * xu
                + (b + a * mean_flow[1]) * yl
                + (b - a * mean_flow[1]) * yu
                + (b + a * mean_flow[2]) * zl
                + (b - a * mean_flow[2]) * zu
                - a * coupling[f]
            )


def layer_kernel(
    cfg,
    fields_hbm, stiff_hbm, ed_hbm, x1_hbm, x2_hbm, w_hbm, lw_hbm, lb_hbm, mix_hbm, bias_hbm,
    out,
    state, stiff, xs, xr, ys, yr, pairs, filt, ed, x1, x2, wv, lw, lb, mix, bias_row, wide_lift,
    lift, table, p_send, p_recv, p2, r2, q3, r3, c4, r4, rr, ii, mf, r5, r6, s7, r7,
    local, hs, hr, s1s, s1r, s2s, s2r, s3s, s3r, s4s, s4r, s5s, s5r, s6s, s6r, s7s, s7r,
):
    G, H, A, C, CB, KB, OB, KZ, NZL, XL, YL = cfg
    Q = 2 * MY
    NX, NY = 2 * XL, 2 * YL
    gx, gx_peers = peers("gx")
    gy, gy_peers = peers("gy")
    ga = lax.axis_index("ga")
    other = lax.rem(ga + 1, A)
    barrier = pltpu.get_barrier_semaphore()
    for axis, group in (("gx", gx_peers), ("gy", gy_peers)):
        for _, peer, _ in group:
            pl.semaphore_signal(barrier, inc=1, device_id={axis: peer}, device_id_type=MESH)
    pl.semaphore_signal(barrier, inc=1, device_id={"ga": other}, device_id_type=MESH)
    loads = [
        pltpu.make_async_copy(source, target, local.at[n])
        for n, (source, target) in enumerate(
            (
                (fields_hbm, state.at[0, :, pl.ds(1, NZL)]),
                (stiff_hbm, stiff),
                (ed_hbm.at[gy], ed),
                (x1_hbm, x1),
                (x2_hbm, x2),
                (w_hbm, wv),
                (lw_hbm, lw),
                (lb_hbm, lb),
                (mix_hbm, mix),
                (bias_hbm, bias_row),
            )
        )
    ]
    for load in loads:
        load.start()

    NCH, NZC = MODE_CHUNKS, DEPTH_CHUNKS
    KC = KZ // NCH
    W = KC * Q
    ZC = NZL // NZC
    NZ = NZL * A

    def own(values):
        picked = jnp.float32(values[0])
        for n in range(1, A):
            picked = jnp.where(ga == n, jnp.float32(values[n]), picked)
        return picked

    def build_table():
        loads[2].wait()
        e, d = ed[0], ed[1]
        for z in range(NZL):
            for k in range(A * KZ):
                v = [2.0 * math.pi * ((k * (n * NZL + z)) % NZ) / NZ for n in range(A)]
                block = e * own([math.cos(x) for x in v]) + d * own([math.sin(x) for x in v])
                table[k // KC, z * YL : (z + 1) * YL, (k % KC) * Q : (k % KC + 1) * Q] = block.astype(bf16)

    spread = jnp.where(
        lax.broadcasted_iota(jnp.int32, (C * XL, C), 0) // XL
        == lax.broadcasted_iota(jnp.int32, (C * XL, C), 1),
        1.0,
        0.0,
    )

    def tall(values):
        return jnp.sum(spread * values, axis=1, keepdims=True)

    def build_lift():
        for n in (6, 7):
            loads[n].wait()
        for f in range(6):
            values = lw[f : f + 1, :] if f < 5 else lb[...]
            wide_lift[f] = jnp.broadcast_to(tall(values), (C * XL, YL))

    loads[0].wait()
    eye = lax.broadcasted_iota(jnp.int32, (NZL * NX, NZL * NX), 0) == lax.broadcasted_iota(
        jnp.int32, (NZL * NX, NZL * NX), 1
    )
    for t in range(STEPS):
        now = state.at[t]
        for side, (edge_x, edge_y) in enumerate(((NX - 1, NY - 1), (0, 0))):
            for f in range(5):
                for z in range(NZL):
                    xs[side, f, z : z + 1, :] = now[f, z + 1, edge_x : edge_x + 1, :]
                column = now[f, 1 : NZL + 1, :, edge_y : edge_y + 1].reshape(NZL * NX, 1)
                ys[side, f : f + 1, :] = jnp.sum(
                    jnp.where(eye, jnp.broadcast_to(column, eye.shape), 0.0), axis=0, keepdims=True
                )
        if t == 0:
            pl.semaphore_wait(barrier, (G - 1) + (H - 1) + 1)
        copies = []
        for side in range(2):
            shift = 1 if side == 0 else -1
            tx, ty, ta = (
                lax.rem(lax.axis_index(n) + lax.axis_size(n) + shift, lax.axis_size(n))
                for n in ("gx", "gy", "ga")
            )
            sems = (hs.at[t], hr.at[t])
            copies.append(remote(ys.at[side], yr.at[t, side], sems, side, "gy", ty))
            copies.append(remote(xs.at[side], xr.at[t, side], sems, 2 + side, "gx", tx))
            plane, halo = (NZL, 0) if side == 0 else (1, NZL + 1)
            copies.append(remote(now.at[:, plane], now.at[:, halo], sems, 4 + side, "ga", ta))
        for one in copies:
            one.start()
        if t == 0:
            build_table()
            loads[1].wait()
        if t == STEPS - 1:
            build_lift()
        for one in copies:
            one.wait()
        stencil_step(now, state.at[t + 1], stiff, xr.at[t], yr.at[t], (NZL, NX, NY))

    both = lax.broadcasted_iota(jnp.int32, (NY, YL), 0) // 2 == lax.broadcasted_iota(
        jnp.int32, (NY, YL), 1
    )
    both = jnp.where(both, 1.0, 0.0)
    for f in range(5):
        pairs[f] = lax.dot_general(
            state[STEPS, f, 1 : NZL + 1].reshape(NZL * NX, NY),
            both,
            (((1,), (0,)), ((), ())),
            precision=highest,
            preferred_element_type=f32,
        )
        for z in range(NZL):
            filt[f, z] = 0.25 * (
                pairs[f, pl.ds(z * NX, XL, stride=2), :] + pairs[f, pl.ds(z * NX + 1, XL, stride=2), :]
            )

    def lift_two(pair, carry):
        rows = pl.ds(pl.multiple_of(pair * 2 * XL, 2 * XL), 2 * XL)
        weights = [wide_lift[f, rows, :] for f in range(6)]
        for z in range(NZL):
            v = weights[5]
            for f in range(5):
                v = v + jnp.concatenate([filt[f, z], filt[f, z]], axis=0) * weights[f]
            lift[rows, z * YL : (z + 1) * YL] = gelu(v).astype(bf16)
        return carry

    lax.fori_loop(0, C // 2, lift_two, 0)

    stage1 = []
    for h in range(NCH):
        p_send[h] = dot(lift[...], table[other * NCH + h]).astype(bf16)
        stage1.append(remote(p_send.at[h], p_recv.at[h], (s1s, s1r), h, "ga", other))
        stage1[-1].start()

    stage2 = []
    for h in range(NCH):
        mine = dot(lift[...], table[ga * NCH + h])
        stage1[h].wait()
        p2[h] = (mine + p_recv[h].astype(f32)).astype(bf16).reshape(p2.shape[1:])
        group = []
        for n, peer, _ in gx_peers:
            slot = h * (G - 1) + n - 1
            group.append(remote(p2.at[h, peer], r2.at[h, gx], (s2s, s2r), slot, "gx", peer))
            group[-1].start()
        r2[h, gx] = p2[h, gx]
        stage2.append(group)

    loads[3].wait()
    stage3 = []
    for h in range(NCH):
        for one in stage2[h]:
            one.wait()
        v = r2[h].reshape(C * XL, W)
        vs = swapped(v.astype(f32)).astype(bf16)
        q3[h] = dot(x1[...], jnp.concatenate([v, vs], axis=0)).astype(bf16).reshape(q3.shape[1:])
        group = []
        for n, peer, _ in gy_peers:
            slot = h * (H - 1) + n - 1
            group.append(remote(q3.at[h, peer], r3.at[h, n - 1], (s3s, s3r), slot, "gy", peer))
            group[-1].start()
        stage3.append(group)

    stage4 = []
    for h in range(NCH):
        acc = q3[h, gy].astype(f32)
        for n, one in enumerate(stage3[h]):
            one.wait()
            acc = acc + r3[h, n].astype(f32)
        c4[h] = acc.astype(bf16)
        group = []
        for n, peer, _ in gx_peers:
            slot = h * (G - 1) + n - 1
            group.append(remote(c4.at[h], r4.at[h, gx], (s4s, s4r), slot, "gx", peer))
            group[-1].start()
        r4[h, gx] = c4[h]
        stage4.append(group)

    loads[5].wait()
    low = lax.broadcasted_iota(jnp.int32, (C * KB, Q), 1) < MY
    stage5 = []
    stage6 = []
    for h in range(NCH):
        for one in stage4[h]:
            one.wait()
        v = r4[h].reshape(C * KB, W).astype(f32)
        for k in range(KC):
            part = v[:, k * Q : (k + 1) * Q]
            turned = pltpu.roll(part, MY, 1)
            rr[h * KC + k] = jnp.where(low, part, turned)
            ii[h * KC + k] = jnp.where(low, turned, part)

        def mix_one(kx, carry):
            for k in range(KC):
                a = jnp.zeros((OB, Q), f32)
                b = jnp.zeros((OB, Q), f32)
                for c in range(C):
                    w = wv[h * KC + k, kx, c]
                    a = a + w * rr[h * KC + k, pl.ds(c * KB + kx, 1), :]
                    b = b + w * ii[h * KC + k, pl.ds(c * KB + kx, 1), :]
                mf[h, kx, :, k * Q : (k + 1) * Q] = a - swapped(b)
            return carry

        lax.fori_loop(0, KB, mix_one, 0)
        r5[h, gy] = mf[h].reshape(KB * OB, W).astype(bf16)
        group = []
        for n, peer, _ in gy_peers:
            slot = h * (H - 1) + n - 1
            group.append(remote(r5.at[h, gy], r5.at[h, gy], (s5s, s5r), slot, "gy", peer))
            group[-1].start()
        stage5.append(group)
        stage6.append([remote(r5.at[h, gy], r6.at[h, gy], (s6s, s6r), h * H, "ga", other)])
        stage6[h][0].start()

    loads[8].wait()
    loads[9].wait()
    bias = tall(bias_row[...])
    wide = dot(spread.astype(bf16), mix[...], ((1,), (1,))).astype(bf16)
    wide = dot(wide, spread.astype(bf16), ((1,), (1,)))
    same = lax.rem(lax.broadcasted_iota(jnp.int32, wide.shape, 0), XL) == lax.rem(
        lax.broadcasted_iota(jnp.int32, wide.shape, 1), XL
    )
    mixk = jnp.where(same, wide, 0.0).astype(bf16)

    loads[4].wait()
    rows = H * KB * OB

    def back(v):
        v = v.reshape(rows, W)
        vs = swapped(v.astype(f32)).astype(bf16)
        return dot(x2[...], jnp.concatenate([v, vs], axis=0)).astype(bf16)

    modes = []
    for h in range(NCH):
        for (n, _, source), one in zip(gy_peers, stage5[h]):
            one.wait_recv()
            stage6[h].append(
                remote(r5.at[h, source], r6.at[h, source], (s6s, s6r), h * H + n, "ga", other)
            )
            stage6[h][-1].start()
        modes.append((ga * NCH + h, back(r5[h])))
    for h in range(NCH):
        for one in stage5[h]:
            one.wait_send()
        for one in stage6[h]:
            one.wait()
        modes.append((other * NCH + h, back(r6[h])))

    stage7 = []
    for j in range(NZC):
        span = slice(j * ZC * YL, (j + 1) * ZC * YL)
        spec = dot(modes[0][1], table[modes[0][0], span, :], ((1,), (1,)))
        for at, y in modes[1:]:
            spec = spec + dot(y, table[at, span, :], ((1,), (1,)))
        s7[j] = spec.astype(bf16).reshape(s7.shape[1:])
        group = []
        for n, peer, _ in gx_peers:
            slot = j * (G - 1) + n - 1
            group.append(remote(s7.at[j, peer], r7.at[j, gx], (s7s, s7r), slot, "gx", peer))
            group[-1].start()
        r7[j, gx] = s7[j, gx]
        stage7.append(group)
    for j in range(NZC):
        span = slice(j * ZC * YL, (j + 1) * ZC * YL)
        direct = dot(mixk, lift[:, span]) + bias
        for one in stage7[j]:
            one.wait()
        both = gelu(direct + r7[j].reshape(C * XL, ZC * YL).astype(f32)).astype(bf16)
        for z in range(ZC):
            out[j * ZC + z] = both[:, z * YL : (z + 1) * YL].reshape(C, XL, YL)


def east_tables(G, H, XL, C):
    CB, KB, OB = C // G, MX // H, C // G
    length = G * XL
    k = np.arange(MX) - MX // 2
    ang = 2.0 * np.pi * ((k[:, None] * np.arange(length)[None, :]) % length) / length
    scale = 1.0 / math.sqrt(length)
    cos, sin = np.cos(ang) * scale, np.sin(ang) * scale
    cos[np.abs(cos) < 1e-12] = 0.0
    sin[np.abs(sin) < 1e-12] = 0.0

    def forward(t):
        t = t.reshape(H, KB, G, XL)
        full = np.einsum("hkgx,cd->hckgdx", t, np.eye(CB))
        return full.reshape(H * CB * KB, G * CB * XL)

    def inverse(t):
        t = t.reshape(H, KB, G, XL)
        full = np.einsum("hkgx,op->goxhkp", t, np.eye(OB))
        return full.reshape(G * OB * XL, H * KB * OB)

    x1 = np.concatenate([forward(cos), forward(sin)], axis=1)
    x2 = np.concatenate([inverse(cos), -inverse(sin)], axis=1)
    return jnp.asarray(x1, bf16), jnp.asarray(x2, bf16)


def north_tables(H, YL, NZ):
    length = H * YL
    n = np.arange(MY) - MY // 2
    u = 2.0 * np.pi * ((np.arange(length)[:, None] * n[None, :]) % length) / length
    scale = 1.0 / math.sqrt(length * NZ)
    cu, su = np.cos(u) * scale, np.sin(u) * scale
    both = np.stack([np.concatenate([cu, -su], axis=1), np.concatenate([-su, -cu], axis=1)])
    return jnp.asarray(both.reshape(2, H, YL, 2 * MY).transpose(1, 0, 2, 3), f32)


def shards(fields, stiffness, lift_weight, lift_bias, mix_weight, spectral_weight, output_bias):
    G, H, A = (lax.axis_size(n) for n in ("gx", "gy", "ga"))
    _, NZL, NX, NY = fields.shape
    XL, YL = NX // 2, NY // 2
    C = lift_weight.shape[1]
    CB, KB, OB, KZ, Q = C // G, MX // H, C // G, MZ // A, 2 * MY
    NZ = NZL * A
    x1, x2 = east_tables(G, H, XL, C)
    ed = north_tables(H, YL, NZ)
    cfg = (G, H, A, C, CB, KB, OB, KZ, NZL, XL, YL)
    vmem = pl.BlockSpec(memory_space=pltpu.VMEM)
    hbm = pl.BlockSpec(memory_space=pltpu.HBM)
    NCH, NZC = MODE_CHUNKS, DEPTH_CHUNKS
    W = KZ // NCH * Q
    ZW = NZL // NZC * YL
    dma = pltpu.SemaphoreType.DMA
    V = pltpu.VMEM
    return pl.pallas_call(
        functools.partial(layer_kernel, cfg),
        out_shape=jax.ShapeDtypeStruct((NZL, C, XL, YL), bf16),
        in_specs=[hbm] * 10,
        out_specs=vmem,
        scratch_shapes=[
            V((STEPS + 1, 5, NZL + 2, NX, NY), f32),
            V((NZL, NX, NY), f32),
            V((2, 5, NZL, NY), f32),
            V((STEPS, 2, 5, NZL, NY), f32),
            V((2, 5, NZL * NX), f32),
            V((STEPS, 2, 5, NZL * NX), f32),
            V((5, NZL * NX, YL), f32),
            V((5, NZL, XL, YL), f32),
            V(ed.shape[1:], f32),
            V(x1.shape, bf16),
            V(x2.shape, bf16),
            V(spectral_weight.shape, f32),
            V(lift_weight.shape, f32),
            V((1, C), f32),
            V(mix_weight.shape, bf16),
            V((1, C), f32),
            V((6, C * XL, YL), f32),
            V((C * XL, NZL * YL), bf16),
            V((A * NCH, NZL * YL, W), bf16),
            V((NCH, C * XL, W), bf16),
            V((NCH, C * XL, W), bf16),
            V((NCH, G, CB * XL, W), bf16),
            V((NCH, G, CB * XL, W), bf16),
            V((NCH, H, CB * KB, W), bf16),
            V((NCH, H - 1, CB * KB, W), bf16),
            V((NCH, CB * KB, W), bf16),
            V((NCH, G, CB * KB, W), bf16),
            V((KZ, C * KB, Q), f32),
            V((KZ, C * KB, Q), f32),
            V((NCH, KB, OB, W), f32),
            V((NCH, H, KB * OB, W), bf16),
            V((NCH, H, KB * OB, W), bf16),
            V((NZC, G, OB * XL, ZW), bf16),
            V((NZC, G, OB * XL, ZW), bf16),
            dma((10,)),
            dma((STEPS, 6)), dma((STEPS, 6)),
            dma((NCH,)), dma((NCH,)),
            dma((NCH * (G - 1),)), dma((NCH * (G - 1),)),
            dma((NCH * (H - 1),)), dma((NCH * (H - 1),)),
            dma((NCH * (G - 1),)), dma((NCH * (G - 1),)),
            dma((NCH * (H - 1),)), dma((NCH * (H - 1),)),
            dma((NCH * H,)), dma((NCH * H,)),
            dma((NZC * (G - 1),)), dma((NZC * (G - 1),)),
        ],
        compiler_params=pltpu.CompilerParams(collective_id=0, has_side_effects=True, vmem_limit_bytes=67043328),
    )(
        fields, stiffness, ed, x1, x2, spectral_weight,
        lift_weight, lift_bias[None, :], mix_weight, output_bias[None, :],
    )


def solution(mesh):
    placed = (
        P(None, "ga", "gx", "gy"),
        P("ga", "gx", "gy"),
        P(),
        P(),
        P(),
        P("ga", "gy", None, "gx", None),
        P(),
    )
    return jax.shard_map(
        shards, mesh=mesh, in_specs=placed, out_specs=P("ga", None, "gx", "gy"), check_vma=False
    )
```
